32 devices in a mesh: clu: 8 (over z, x), grp: 4 (over y, core).
Axes of the slice: x: 2, y: 2, z: 4, core: 2. Of those that a mesh axis runs over, the one named last changes fastest.
Arguments:
- document_vectors: bfloat16 [8192, 768], P(('clu', 'grp')), may hold values from -100 to 100
- group_label: int32 [8192], P(('clu', 'grp')), may hold values from 0 to 7, as said below
- within_group_position: int32 [8192], P(('clu', 'grp')), may hold values from 0 to 8191, each once
- bucket_boundaries: int32 [128], replicated, may hold values from 0 to 1008, as said below
- threshold_smoothness: int32 [1], replicated, may hold values from 20 to 59
- desired_retention_share: int32 [1], replicated, may hold values from 300 to 700
Outputs:
- nearest: float32 [8192], P(('clu', 'grp'))
- keep_weight: float32 [8192], P(('clu', 'grp'))
The draws below stay inside these ranges and needn't reach their ends.
Inputs may be any that keep to these rules, and one draw needn't show every extreme that they name: `group_label`: among the 256 documents of one device (aligned blocks of the encoder order) no cluster appears more than 64 times, and on every device exactly three clusters appear 64 times. `bucket_boundaries`: strictly increasing.
All inputs are finite; a program needn't handle non-finite values.
Results may differ from the reference program's by a relative error of at most 0.0003.
The reference program's roundings to bfloat16 on the way count: a program that leaves them out, or rounds other values in their place, can miss the bound.
Values may be sent and summed in bfloat16 or wider, within the bound.
No kernel may reach another device: no remote copies, remote signals or barrier semaphores. Data moves between devices by JAX's collectives and lax.ppermute only.
A program may use at most 64 MiB of HBM per device.

```python
import jax
import jax.numpy as jnp
from jax import lax

E = 768
DOC_DEV = 256
NBIN = 128
NCLUS = 8
SEND = 64
N_DOC = 8192
DEVICES = 32


def cluster_table(key):
    base_key = jax.random.fold_in(key, 11)
    key_bias, score_for_key, key_rest, key_shuffle = jax.random.split(base_key, 4)
    block_count = N_DOC // DOC_DEV
    favored = jnp.where(jax.random.permutation(key_bias, NCLUS) < 4, 256, 0).astype(jnp.int32)
    scores = jax.random.randint(score_for_key, (block_count, NCLUS), 0, 512).astype(jnp.int32) + favored[None, :]
    scores = scores * NCLUS + jnp.arange(NCLUS, dtype=jnp.int32)[None, :]
    top_vals, hot_ids = lax.top_k(scores, 3)
    hot_ids = hot_ids.astype(jnp.int32)
    is_hot = jnp.sum((hot_ids[:, :, None] == jnp.arange(NCLUS, dtype=jnp.int32)[None, None, :]).astype(jnp.int32), axis=1)
    others = jnp.argsort(is_hot * NCLUS + jnp.arange(NCLUS, dtype=jnp.int32)[None, :], axis=1).astype(jnp.int32)[:, :NCLUS - 3]
    picks = jax.random.randint(key_rest, (block_count, SEND), 0, NCLUS - 3).astype(jnp.int32)
    rest_ids = jnp.take_along_axis(others, picks, axis=1)
    hot_rows = jnp.repeat(hot_ids, SEND, axis=1)
    assigned = jnp.concatenate([hot_rows, rest_ids], axis=1)
    shuffle_keys = jax.random.split(key_shuffle, block_count)
    shuffled = jax.vmap(lambda one_key, one_row: jax.random.permutation(one_key, one_row))(shuffle_keys, assigned)
    return shuffled.reshape(N_DOC).astype(jnp.int32)


def draw_group_label(key, part):
    return cluster_table(key)


def draw_document_vectors(key, part):
    cluster_ids = cluster_table(key)
    emb_key = jax.random.fold_in(key, 23)
    key_center, key_coef, key_noise = jax.random.split(emb_key, 3)
    centers = jnp.clip(jax.random.normal(key_center, (NCLUS, E), jnp.float32), -4.0, 4.0)
    coef = jax.random.uniform(key_coef, (N_DOC, 1), jnp.float32, 0.3, 1.5)
    noise = jnp.clip(jax.random.normal(key_noise, (N_DOC, E), jnp.float32), -4.0, 4.0)
    values = coef * centers[cluster_ids] + noise
    return values.astype(jnp.bfloat16)


def draw_bucket_boundaries(key, part):
    edge_key = jax.random.fold_in(key, 37)
    key_start, key_steps = jax.random.split(edge_key)
    first_edge = jax.random.randint(key_start, (1,), 0, 120).astype(jnp.int32)
    edge_steps = jax.random.randint(key_steps, (NBIN - 2,), 4, 8).astype(jnp.int32)
    lower_edges = jnp.concatenate([first_edge, first_edge + jnp.cumsum(edge_steps)]).astype(jnp.int32)
    top_edge = jnp.full((1,), 119 + 7 * (NBIN - 1), jnp.int32)
    return jnp.concatenate([lower_edges, top_edge]).astype(jnp.int32)


def setup_inputs(seed: int = 0) -> dict:
    keys = jax.random.split(jax.random.key(seed), 7)
    document_vectors = draw_document_vectors(jax.random.fold_in(keys[6], 71), 0)
    group_label = draw_group_label(jax.random.fold_in(keys[6], 71), 0)
    within_group_position = jax.random.permutation(keys[2], N_DOC).astype(jnp.int32)
    bucket_boundaries = draw_bucket_boundaries(jax.random.fold_in(keys[6], 71), 0)
    threshold_smoothness = jax.random.randint(keys[4], (1,), 20, 60).astype(jnp.int32)
    desired_retention_share = jax.random.randint(keys[5], (1,), 300, 701).astype(jnp.int32)
    return dict(document_vectors=document_vectors, group_label=group_label, within_group_position=within_group_position, bucket_boundaries=bucket_boundaries, threshold_smoothness=threshold_smoothness, desired_retention_share=desired_retention_share)


def rows_to_unit_norm(document_vectors):
    values = document_vectors.astype(jnp.float32)
    return (values / jnp.sqrt(lax.optimization_barrier(jnp.sum(values * values, axis=-1, keepdims=True)) + 1e-06)).astype(jnp.bfloat16)

def reference(document_vectors, group_label, within_group_position, bucket_boundaries, threshold_smoothness, desired_retention_share):
    unit_rows = rows_to_unit_norm(document_vectors)
    total_docs = group_label.shape[0]
    sort_key = group_label.astype(jnp.int32) * total_docs + within_group_position.astype(jnp.int32)
    order_perm = jnp.argsort(sort_key).astype(jnp.int32)
    sorted_rows = unit_rows[order_perm].astype(jnp.float32)
    clusters_in_order = group_label[order_perm]
    sorted_keys = within_group_position[order_perm]
    block_len = min(512, total_docs)
    window = min(total_docs, SEND * DEVICES + block_len)

    def block_max(block_id):
        start_at = (block_id * block_len).astype(jnp.int32)
        window_lo = jnp.clip(start_at + block_len - window, 0, total_docs - window).astype(jnp.int32)
        row_vals = lax.dynamic_slice_in_dim(sorted_rows, start_at, block_len, 0)
        row_clus = lax.dynamic_slice_in_dim(clusters_in_order, start_at, block_len, 0)
        row_keys = lax.dynamic_slice_in_dim(sorted_keys, start_at, block_len, 0)
        col_vals = lax.dynamic_slice_in_dim(sorted_rows, window_lo, window, 0)
        col_clus = lax.dynamic_slice_in_dim(clusters_in_order, window_lo, window, 0)
        col_keys = lax.dynamic_slice_in_dim(sorted_keys, window_lo, window, 0)
        tile_sims = jnp.dot(row_vals, col_vals.T, preferred_element_type=jnp.float32)
        earlier = (col_clus[None, :] == row_clus[:, None]) & (col_keys[None, :] < row_keys[:, None])
        return lax.optimization_barrier(jnp.max(jnp.where(earlier, tile_sims, 0.0), axis=1))
    block_ids = jnp.arange(total_docs // block_len).astype(jnp.int32)
    nearest_sorted = lax.map(block_max, block_ids).reshape(total_docs)
    nearest = jnp.zeros((total_docs,), jnp.float32).at[order_perm].set(nearest_sorted)
    smooth_threshold = threshold_smoothness[0].astype(jnp.float32) / 1000.0
    edge_vals = bucket_boundaries.astype(jnp.float32) / 1000.0
    rate_val = desired_retention_share[0].astype(jnp.float32) / 1000.0
    above_sum = lax.optimization_barrier(jnp.sum(jax.nn.sigmoid((nearest[:, None] - edge_vals[None, :]) / smooth_threshold), axis=0))
    below_frac = 1.0 - above_sum / total_docs
    cutoff = edge_vals[0] + jnp.sum((edge_vals[1:] - edge_vals[:-1]) * jax.nn.sigmoid((rate_val - below_frac[:-1]) / 0.05))
    keep_weight = jax.nn.sigmoid((cutoff - nearest) / smooth_threshold)
    return (nearest, keep_weight)
```

```python
import functools

import jax
import jax.numpy as jnp
from jax import lax
from jax.experimental import pallas as pl
from jax.experimental.pallas import tpu as pltpu
from jax.sharding import PartitionSpec as P

AXES = ("clu", "grp")
KEY_ROWS = 8


def vmem():
    return pl.BlockSpec(memory_space=pltpu.VMEM)


def smem():
    return pl.BlockSpec(memory_space=pltpu.SMEM)


def flat_lanes(ref):
    return jnp.concatenate([ref[i : i + 1, :] for i in range(ref.shape[0])], axis=1)


def prep_kernel(rows_ref, label_ref, pos_ref, out_ref):
    docs, width = rows_ref.shape
    values = rows_ref[...].astype(jnp.float32)
    total = jnp.sum(values * values, axis=1, keepdims=True)
    out_ref[0:docs, :] = (values / jnp.sqrt(total + 1e-06)).astype(jnp.bfloat16)
    label = flat_lanes(label_ref)
    pos = flat_lanes(pos_ref)
    high = pos >> 8
    low = pos & 255
    key = jnp.concatenate([label, high, low], axis=1).astype(jnp.float32)
    rest = width - key.shape[1]
    if rest:
        key = jnp.concatenate([key, jnp.zeros((1, rest), jnp.float32)], axis=1)
    out_ref[docs:, :] = jnp.broadcast_to(key, (KEY_ROWS, width)).astype(jnp.bfloat16)


def keys_of(ref, docs, total_docs):
    key = ref[docs : docs + KEY_ROWS, :].astype(jnp.float32)
    start = key[:, 0:docs] * float(total_docs)
    return start + key[:, docs : 2 * docs] * 256.0 + key[:, 2 * docs : 3 * docs], start


def match_kernel(total_docs, docs, n_rows, n_cols, *refs):
    row_refs = refs[:n_rows]
    col_refs = refs[n_rows : n_rows + n_cols]
    out_ref = refs[n_rows + n_cols]
    row_keys = []
    for ref in row_refs:
        key, start = keys_of(ref, docs, total_docs)
        row_keys.append((key[0:1, :], start[0:1, :]))
    best = [jnp.zeros((1, docs), jnp.float32) for _ in row_refs]
    for col in col_refs:
        key, _ = keys_of(col, docs, total_docs)
        key = jnp.transpose(key)[:, 0:1]
        for i, row in enumerate(row_refs):
            sims = lax.dot_general(
                col[0:docs, :],
                row[0:docs, :],
                (((1,), (1,)), ((), ())),
                preferred_element_type=jnp.float32,
            )
            earlier = (key < row_keys[i][0]) & (key >= row_keys[i][1])
            best[i] = jnp.maximum(
                best[i], jnp.max(jnp.where(earlier, sims, 0.0), axis=0, keepdims=True)
            )
    for i in range(n_rows):
        out_ref[i : i + 1, :] = best[i]


def match(rows, cols, docs, total_docs):
    width = rows[0].shape[1]
    flops = 2 * len(rows) * len(cols) * docs * docs * width
    return pl.pallas_call(
        functools.partial(match_kernel, total_docs, docs, len(rows), len(cols)),
        out_shape=jax.ShapeDtypeStruct((len(rows), docs), jnp.float32),
        in_specs=[vmem()] * (len(rows) + len(cols)),
        out_specs=vmem(),
        cost_estimate=pl.CostEstimate(
            flops=flops, bytes_accessed=2 * docs * width * (len(rows) + len(cols)), transcendentals=0
        ),
        name="match",
    )(*rows, *cols)


def sigmoid(x):
    return 1.0 / (1.0 + jnp.exp(-x))


def hist_kernel(near_ref, edge_ref, smooth_ref, out_ref):
    bins = edge_ref.shape[1]
    tau = smooth_ref[0].astype(jnp.float32) / 1000.0
    edges = jnp.broadcast_to(edge_ref[...].astype(jnp.float32) / 1000.0, (8, bins))
    edges = jnp.transpose(edges)[:, 0:1]
    total = None
    for i in range(near_ref.shape[0]):
        term = sigmoid((near_ref[i : i + 1, :] - edges) / tau)
        total = term if total is None else total + term
    out_ref[...] = jnp.sum(jnp.transpose(total), axis=0, keepdims=True)


def final_kernel(total_docs, above_ref, near_ref, edge_ref, smooth_ref, rate_ref, out_ref):
    bins = edge_ref.shape[1]
    tau = smooth_ref[0].astype(jnp.float32) / 1000.0
    rate = rate_ref[0].astype(jnp.float32) / 1000.0
    edges = edge_ref[...].astype(jnp.float32) / 1000.0
    step = jnp.concatenate([edges[:, 1:], edges[:, bins - 1 :]], axis=1) - edges
    below = 1.0 - above_ref[...] / float(total_docs)
    cutoff = edges[:, 0:1] + jnp.sum(
        step * sigmoid((rate - below) / 0.05), axis=1, keepdims=True
    )
    keep = sigmoid((cutoff - near_ref[...]) / tau)
    for i in range(out_ref.shape[0]):
        out_ref[i : i + 1, :] = keep[:, i * 128 : (i + 1) * 128]


def body(
    row_bits,
    col_bits,
    owners,
    group_size,
    document_vectors,
    group_label,
    within_group_position,
    bucket_boundaries,
    threshold_smoothness,
    desired_retention_share,
):
    docs, width = document_vectors.shape
    devices = owners * group_size
    total_docs = docs * devices
    bins = bucket_boundaries.shape[0]

    def swap(value, bit):
        return lax.ppermute(value, AXES, [(d, d ^ bit) for d in range(devices)])

    own = pl.pallas_call(
        prep_kernel,
        out_shape=jax.ShapeDtypeStruct((docs + KEY_ROWS, width), jnp.bfloat16),
        in_specs=[vmem()] * 3,
        out_specs=vmem(),
        name="prep",
    )(
        document_vectors,
        group_label.reshape(docs // 128, 128),
        within_group_position.reshape(docs // 128, 128),
    )
    rows = {0: own}
    cols = {0: own}
    for bit in row_bits:
        rows.update({mask | bit: swap(block, bit) for mask, block in list(rows.items())})
    for bit in col_bits:
        cols.update({mask | bit: swap(block, bit) for mask, block in list(cols.items())})
    row_masks = sorted(rows)
    near = match([rows[m] for m in row_masks], [cols[m] for m in sorted(cols)], docs, total_docs)
    for bit in row_bits:
        other = swap(near, bit)
        index = [row_masks.index(m ^ bit) for m in row_masks]
        near = jnp.maximum(near, jnp.concatenate([other[i : i + 1] for i in index], axis=0))
    edges = bucket_boundaries.reshape(1, bins)
    above = pl.pallas_call(
        hist_kernel,
        out_shape=jax.ShapeDtypeStruct((1, bins), jnp.float32),
        in_specs=[vmem(), vmem(), smem()],
        out_specs=vmem(),
        name="hist",
    )(near, edges, threshold_smoothness)
    for bit in reversed(col_bits):
        above = above + swap(above, bit)
    nearest = near[0:1]
    keep = pl.pallas_call(
        functools.partial(final_kernel, total_docs),
        out_shape=jax.ShapeDtypeStruct((docs // 128, 128), jnp.float32),
        in_specs=[vmem(), vmem(), vmem(), smem(), smem()],
        out_specs=vmem(),
        name="final",
    )(above, nearest, edges, threshold_smoothness, desired_retention_share)
    return nearest.reshape(docs), keep.reshape(docs)


def solution(mesh):
    owners = mesh.shape["clu"]
    group_size = mesh.shape["grp"]
    core_bit = 1
    grp_bits = [1 << b for b in range(1, group_size.bit_length() - 1)]
    clu_bits = [group_size << b for b in range(owners.bit_length() - 1)]
    row_bits = [clu_bits[-1]] + grp_bits
    col_bits = [clu_bits[-2]] + clu_bits[:-2] + [core_bit]
    in_specs = (P(AXES, None), P(AXES), P(AXES), P(), P(), P())
    out_specs = (P(AXES), P(AXES))
    return jax.shard_map(
        functools.partial(body, row_bits, col_bits, owners, group_size),
        mesh=mesh,
        in_specs=in_specs,
        out_specs=out_specs,
        check_vma=False,
    )
```

```python
import functools

import jax
import jax.numpy as jnp
from jax import lax
from jax.experimental import pallas as pl
from jax.experimental.pallas import tpu as pltpu
from jax.sharding import PartitionSpec as P

AXES = ("clu", "grp")
KEY_ROWS = 8


def vmem():
    return pl.BlockSpec(memory_space=pltpu.VMEM)


def flat_lanes(ref):
    return jnp.concatenate([ref[i : i + 1, :] for i in range(ref.shape[0])], axis=1)


def prep_kernel(rows_ref, label_ref, pos_ref, out_ref):
    docs, width = rows_ref.shape
    values = rows_ref[...].astype(jnp.float32)
    total = jnp.sum(values * values, axis=1, keepdims=True)
    out_ref[0:docs, :] = (values / jnp.sqrt(total + 1e-06)).astype(jnp.bfloat16)
    label = flat_lanes(label_ref)
    pos = flat_lanes(pos_ref)
    high = pos >> 8
    low = pos & 255
    key = jnp.concatenate([label, high, low], axis=1).astype(jnp.float32)
    rest = width - key.shape[1]
    if rest:
        key = jnp.concatenate([key, jnp.zeros((1, rest), jnp.float32)], axis=1)
    out_ref[docs:, :] = jnp.broadcast_to(key, (KEY_ROWS, width)).astype(jnp.bfloat16)


def keys_of(ref, docs, total_docs):
    key = ref[docs : docs + KEY_ROWS, :].astype(jnp.float32)
    start = key[:, 0:docs] * float(total_docs)
    return start + key[:, docs : 2 * docs] * 256.0 + key[:, 2 * docs : 3 * docs], start


def match_kernel(total_docs, docs, plans, has_start, *refs):
    out_ref = refs[-1]
    blocks = refs[1:-1] if has_start else refs[:-1]

    def run(plan):
        keys = {}

        def col_key(c):
            if c not in keys:
                key, _ = keys_of(blocks[c], docs, total_docs)
                keys[c] = jnp.transpose(key)[:, 0:1]
            return keys[c]

        for i, (r, cols) in enumerate(plan):
            best = refs[0][i : i + 1, :] if has_start else jnp.zeros((1, docs), jnp.float32)
            if cols:
                row = blocks[r]
                row_key, start = keys_of(row, docs, total_docs)
                row_key, start = row_key[0:1, :], start[0:1, :]
                for c in cols:
                    sims = lax.dot_general(
                        blocks[c][0:docs, :],
                        row[0:docs, :],
                        (((1,), (1,)), ((), ())),
                        preferred_element_type=jnp.float32,
                    )
                    key = col_key(c)
                    earlier = (key < row_key) & (key >= start)
                    best = jnp.maximum(
                        best, jnp.max(jnp.where(earlier, sims, 0.0), axis=0, keepdims=True)
                    )
            out_ref[i : i + 1, :] = best

    if len(plans) == 1:
        run(plans[0])
    else:
        core = lax.axis_index("grp") & 1
        for k, plan in enumerate(plans):
            pl.when(core == k)(functools.partial(run, plan))


def match(blocks, plans, docs, total_docs, start=None):
    width = blocks[0].shape[1]
    pairs = max(sum(len(cols) for _, cols in plan) for plan in plans)
    args = list(blocks) if start is None else [start] + list(blocks)
    return pl.pallas_call(
        functools.partial(match_kernel, total_docs, docs, plans, start is not None),
        out_shape=jax.ShapeDtypeStruct((len(plans[0]), docs), jnp.float32),
        in_specs=[vmem()] * len(args),
        out_specs=vmem(),
        cost_estimate=pl.CostEstimate(
            flops=2 * pairs * docs * docs * width,
            bytes_accessed=2 * docs * width * len(blocks),
            transcendentals=0,
        ),
        compiler_params=pltpu.CompilerParams(vmem_limit_bytes=24 << 20),
        name="match",
    )(*args)


def body(
    row_bits,
    col_bits,
    owners,
    group_size,
    document_vectors,
    group_label,
    within_group_position,
    bucket_boundaries,
    threshold_smoothness,
    desired_retention_share,
):
    docs, width = document_vectors.shape
    devices = owners * group_size
    total_docs = docs * devices
    bins = bucket_boundaries.shape[0]

    def send(value, pairs):
        return lax.ppermute(value, AXES, pairs)

    def swap(value, bit):
        return send(value, [(d, d ^ bit) for d in range(devices)])

    def split(value, even_bit, odd_bit):
        pairs = [(d, d ^ (odd_bit if d & 1 else even_bit)) for d in range(devices)]
        return send(value, pairs)

    own = pl.pallas_call(
        prep_kernel,
        out_shape=jax.ShapeDtypeStruct((docs + KEY_ROWS, width), jnp.bfloat16),
        in_specs=[vmem()] * 3,
        out_specs=vmem(),
        compiler_params=pltpu.CompilerParams(vmem_limit_bytes=24 << 20),
        name="prep",
    )(
        document_vectors,
        group_label.reshape(docs // 128, 128),
        within_group_position.reshape(docs // 128, 128),
    )
    if len(row_bits) == 2 and len(col_bits) == 3:
        far, y = row_bits
        z, x, _ = col_bits
        own_s = swap(own, 1)
        a1 = split(own, z, far)
        bx = swap(own, x)
        by = swap(own, y)
        a2 = split(own, far, z)
        bx_s = swap(bx, 1)
        f1 = split(a1, x, y)
        e1 = swap(a1, 1)
        g1 = swap(f1, 1)
        e2 = swap(a2, 1)
        f2 = split(a2, y, x)
        g2 = swap(f2, 1)
        row_masks = [0, y, far, y | far]
        near = match(
            [own, by, own_s, bx, bx_s],
            [[(0, [0, 2, 3, 4]), (1, [0, 2, 3, 4]), (0, []), (0, [])]],
            docs,
            total_docs,
        )
        blocks = [own, by, own_s, bx, bx_s, a1, f1, a2, e1, g1, e2]
        near = match(
            blocks,
            [
                [(0, [5, 6, 10]), (1, [5, 6, 10]), (7, [0, 2, 3, 4, 5, 6, 10]), (0, [])],
                [(0, [7, 8, 9]), (1, [7, 8, 9]), (5, [0, 2, 3, 4, 7, 8, 9]), (6, [0, 2, 3, 4, 7, 8, 9])],
            ],
            docs,
            total_docs,
            near,
        )
        blocks = [own, by, own_s, bx, bx_s, a1, f1, a2, f2, e2]
        near = match(
            blocks,
            [
                [(0, []), (0, []), (0, []), (8, [0, 2, 3, 4, 5, 6, 9])],
                [(0, [8]), (1, [8]), (5, [8]), (6, [8])],
            ],
            docs,
            total_docs,
            near,
        )
        near = match(
            [own, by, a2, f2, g2],
            [
                [(0, [4]), (1, [4]), (2, [4]), (3, [4])],
                [(0, []), (0, []), (0, []), (0, [])],
            ],
            docs,
            total_docs,
            near,
        )
    else:
        rows = {0: own}
        cols = {0: own}
        for bit in row_bits:
            rows.update({mask | bit: swap(block, bit) for mask, block in list(rows.items())})
        for bit in col_bits:
            cols.update({mask | bit: swap(block, bit) for mask, block in list(cols.items())})
        row_masks = sorted(rows)
        col_masks = sorted(cols)
        n = len(row_masks)
        blocks = [rows[m] for m in row_masks] + [cols[m] for m in col_masks]
        plan = [(i, list(range(n, len(blocks)))) for i in range(n)]
        near = match(blocks, [plan], docs, total_docs)
    near = near.reshape(len(row_masks), 1, docs)
    for bit in row_bits:
        other = swap(near, bit)
        index = [row_masks.index(m ^ bit) for m in row_masks]
        near = jnp.maximum(near, jnp.concatenate([other[i : i + 1] for i in index], axis=0))
    tau = threshold_smoothness[0].astype(jnp.float32) / 1000.0
    rate = desired_retention_share[0].astype(jnp.float32) / 1000.0
    edges = bucket_boundaries.astype(jnp.float32) / 1000.0
    above = jnp.sum(
        jax.nn.sigmoid((near.reshape(-1)[None, :] - edges[:, None]) / tau), axis=1
    ).reshape(1, bins)
    for bit in reversed(col_bits):
        above = above + swap(above, bit)
    below = 1.0 - above.reshape(bins) / total_docs
    cutoff = edges[0] + jnp.sum(
        (edges[1:] - edges[:-1]) * jax.nn.sigmoid((rate - below[:-1]) / 0.05)
    )
    nearest = near[0].reshape(docs)
    keep = jax.nn.sigmoid((cutoff - nearest) / tau)
    return nearest, keep


def solution(mesh):
    owners = mesh.shape["clu"]
    group_size = mesh.shape["grp"]
    core_bit = 1
    grp_bits = [1 << b for b in range(1, group_size.bit_length() - 1)]
    clu_bits = [group_size << b for b in range(owners.bit_length() - 1)]
    row_bits = [clu_bits[-1]] + grp_bits
    col_bits = [clu_bits[-2]] + clu_bits[:-2] + [core_bit]
    in_specs = (P(AXES, None), P(AXES), P(AXES), P(), P(), P())
    out_specs = (P(AXES), P(AXES))
    return jax.shard_map(
        functools.partial(body, row_bits, col_bits, owners, group_size),
        mesh=mesh,
        in_specs=in_specs,
        out_specs=out_specs,
        check_vma=False,
    )
```

```python
import functools

import jax
import jax.numpy as jnp
from jax import lax
from jax.experimental import pallas as pl
from jax.experimental.pallas import tpu as pltpu
from jax.sharding import PartitionSpec as P

AXES = ("clu", "grp")
KEY_ROWS = 8


def vmem():
    return pl.BlockSpec(memory_space=pltpu.VMEM)


def smem():
    return pl.BlockSpec(memory_space=pltpu.SMEM)


def prep_kernel(rows_ref, key_ref, out_ref):
    docs = rows_ref.shape[0]
    values = rows_ref[...].astype(jnp.float32)
    total = jnp.sum(values * values, axis=1, keepdims=True)
    out_ref[0:docs, :] = (values / jnp.sqrt(total + 1e-06)).astype(jnp.bfloat16)
    out_ref[docs:, :] = key_ref[...]


def key_rows(label, pos, width):
    key = jnp.concatenate([label, pos >> 8, pos & 255])
    key = jnp.pad(key, (0, width - key.shape[0])).astype(jnp.bfloat16)
    return jnp.broadcast_to(key[None, :], (KEY_ROWS, width))


def keys_of(ref, docs, total_docs):
    key = ref[docs : docs + KEY_ROWS, :].astype(jnp.float32)
    start = key[:, 0:docs] * float(total_docs)
    return start + key[:, docs : 2 * docs] * 256.0 + key[:, 2 * docs : 3 * docs], start


def match_kernel(total_docs, docs, plans, has_start, *refs):
    out_ref = refs[-1]
    blocks = refs[1:-1] if has_start else refs[:-1]

    def run(plan):
        keys = {}

        def col_key(c):
            if c not in keys:
                key, _ = keys_of(blocks[c], docs, total_docs)
                keys[c] = jnp.transpose(key)[:, 0:1]
            return keys[c]

        for i, (r, cols) in enumerate(plan):
            best = refs[0][i : i + 1, :] if has_start else jnp.zeros((1, docs), jnp.float32)
            if cols:
                row = blocks[r]
                row_key, start = keys_of(row, docs, total_docs)
                row_key, start = row_key[0:1, :], start[0:1, :]
                for c in cols:
                    sims = lax.dot_general(
                        blocks[c][0:docs, :],
                        row[0:docs, :],
                        (((1,), (1,)), ((), ())),
                        preferred_element_type=jnp.float32,
                    )
                    key = col_key(c)
                    earlier = (key < row_key) & (key >= start)
                    best = jnp.maximum(
                        best, jnp.max(jnp.where(earlier, sims, 0.0), axis=0, keepdims=True)
                    )
            out_ref[i : i + 1, :] = best

    if len(plans) == 1:
        run(plans[0])
    else:
        core = lax.axis_index("grp") & 1
        for k, plan in enumerate(plans):
            pl.when(core == k)(functools.partial(run, plan))


def match(blocks, plans, docs, total_docs, start=None):
    width = blocks[0].shape[1]
    pairs = max(sum(len(cols) for _, cols in plan) for plan in plans)
    args = list(blocks) if start is None else [start] + list(blocks)
    return pl.pallas_call(
        functools.partial(match_kernel, total_docs, docs, plans, start is not None),
        out_shape=jax.ShapeDtypeStruct((len(plans[0]), docs), jnp.float32),
        in_specs=[vmem()] * len(args),
        out_specs=vmem(),
        cost_estimate=pl.CostEstimate(
            flops=2 * pairs * docs * docs * width,
            bytes_accessed=2 * docs * width * len(blocks),
            transcendentals=0,
        ),
        compiler_params=pltpu.CompilerParams(vmem_limit_bytes=24 << 20),
        name="match",
    )(*args)


def sigmoid(x):
    return 1.0 / (1.0 + jnp.exp(-x))


def final_kernel(total_docs, above_ref, other_ref, near_ref, edge_ref, smooth_ref, rate_ref, nearest_ref, keep_ref):
    bins = edge_ref.shape[1]
    tau = smooth_ref[0].astype(jnp.float32) / 1000.0
    rate = rate_ref[0].astype(jnp.float32) / 1000.0
    edges = edge_ref[...].astype(jnp.float32) / 1000.0
    step = jnp.concatenate([edges[:, 1:], edges[:, bins - 1 :]], axis=1) - edges
    below = 1.0 - (above_ref[...] + other_ref[...]) / float(total_docs)
    cutoff = edges[:, 0:1] + jnp.sum(
        step * sigmoid((rate - below) / 0.05), axis=1, keepdims=True
    )
    near = near_ref[0]
    keep = sigmoid((cutoff - near) / tau)
    for i in range(keep_ref.shape[0]):
        nearest_ref[i : i + 1, :] = near[:, i * 128 : (i + 1) * 128]
        keep_ref[i : i + 1, :] = keep[:, i * 128 : (i + 1) * 128]


def body(
    row_bits,
    col_bits,
    owners,
    group_size,
    document_vectors,
    group_label,
    within_group_position,
    bucket_boundaries,
    threshold_smoothness,
    desired_retention_share,
):
    docs, width = document_vectors.shape
    devices = owners * group_size
    total_docs = docs * devices
    bins = bucket_boundaries.shape[0]

    def send(value, pairs):
        return lax.ppermute(value, AXES, pairs)

    def swap(value, bit):
        return send(value, [(d, d ^ bit) for d in range(devices)])

    def split(value, even_bit, odd_bit):
        pairs = [(d, d ^ (odd_bit if d & 1 else even_bit)) for d in range(devices)]
        return send(value, pairs)

    own = pl.pallas_call(
        prep_kernel,
        out_shape=jax.ShapeDtypeStruct((docs + KEY_ROWS, width), jnp.bfloat16),
        in_specs=[vmem()] * 2,
        out_specs=vmem(),
        compiler_params=pltpu.CompilerParams(vmem_limit_bytes=24 << 20),
        name="prep",
    )(document_vectors, key_rows(group_label, within_group_position, width))
    if len(row_bits) == 2 and len(col_bits) == 3:
        far, y = row_bits
        z, x, _ = col_bits
        own_s = swap(own, 1)
        a1 = split(own, far, z)
        bx = swap(own, x)
        by = swap(own, y)
        a2 = split(own_s, far ^ 1, z ^ 1)
        bx_s = swap(bx, 1)
        f1 = split(a1, x, y)
        e1 = swap(a1, 1)
        g1 = swap(f1, 1)
        e2 = swap(a2, 1)
        f2 = split(a2, y, x)
        g2 = swap(f2, 1)
        row_masks = [0, y, far, y ^ far]
        base = [0, 2, 3, 4]
        near = match(
            [own, by, own_s, bx, bx_s], [[(0, base), (1, base), (0, []), (0, [])]], docs, total_docs
        )
        blocks = [own, by, own_s, bx, bx_s, a1, e1, f1, g1, a2, e2]
        near = match(
            blocks,
            [
                [(0, [5, 8, 10]), (1, [5, 8, 10]), (9, base + [5, 8, 10]), (7, base + [5, 8, 10])],
                [(0, [6, 7, 9]), (1, [6, 7, 9]), (5, base + [6, 7, 9]), (0, [])],
            ],
            docs,
            total_docs,
            near,
        )
        blocks = [own, by, own_s, bx, bx_s, a1, e1, f1, a2, f2]
        near = match(
            blocks,
            [
                [(0, [9]), (1, [9]), (8, [9]), (7, [9])],
                [(0, []), (0, []), (0, []), (9, base + [6, 7, 8])],
            ],
            docs,
            total_docs,
            near,
        )
        near = match(
            [own, by, a1, f2, g2],
            [
                [(0, []), (0, []), (0, []), (0, [])],
                [(0, [4]), (1, [4]), (2, [4]), (3, [4])],
            ],
            docs,
            total_docs,
            near,
        )
    else:
        rows = {0: own}
        cols = {0: own}
        for bit in row_bits:
            rows.update({mask ^ bit: swap(block, bit) for mask, block in list(rows.items())})
        for bit in col_bits:
            cols.update({mask ^ bit: swap(block, bit) for mask, block in list(cols.items())})
        row_masks = sorted(rows)
        col_masks = sorted(cols)
        n = len(row_masks)
        blocks = [rows[m] for m in row_masks] + [cols[m] for m in col_masks]
        plan = [(i, list(range(n, len(blocks)))) for i in range(n)]
        near = match(blocks, [plan], docs, total_docs)
    near = near.reshape(len(row_masks), 1, docs)
    for bit in row_bits:
        other = swap(near, bit)
        index = [row_masks.index(m ^ bit) for m in row_masks]
        near = jnp.maximum(near, jnp.concatenate([other[i : i + 1] for i in index], axis=0))
    tau = threshold_smoothness[0].astype(jnp.float32) / 1000.0
    edges = bucket_boundaries.astype(jnp.float32) / 1000.0
    above = jnp.sum(
        jax.nn.sigmoid((near.reshape(-1)[None, :] - edges[:, None]) / tau), axis=1
    ).reshape(1, bins)
    other = jnp.zeros_like(above)
    for bit in reversed(col_bits):
        above = above + other
        other = swap(above, bit)
    nearest, keep = pl.pallas_call(
        functools.partial(final_kernel, total_docs),
        out_shape=[jax.ShapeDtypeStruct((docs // 128, 128), jnp.float32)] * 2,
        in_specs=[vmem()] * 4 + [smem()] * 2,
        out_specs=[vmem()] * 2,
        compiler_params=pltpu.CompilerParams(vmem_limit_bytes=24 << 20),
        name="final",
    )(
        above,
        other,
        near,
        bucket_boundaries.reshape(1, bins),
        threshold_smoothness,
        desired_retention_share,
    )
    return nearest.reshape(docs), keep.reshape(docs)


def solution(mesh):
    owners = mesh.shape["clu"]
    group_size = mesh.shape["grp"]
    core_bit = 1
    grp_bits = [1 << b for b in range(1, group_size.bit_length() - 1)]
    clu_bits = [group_size << b for b in range(owners.bit_length() - 1)]
    row_bits = [bit | core_bit for bit in [clu_bits[-1]] + grp_bits]
    col_bits = [bit | core_bit for bit in [clu_bits[-2]] + clu_bits[:-2]] + [core_bit]
    in_specs = (P(AXES, None), P(AXES), P(AXES), P(), P(), P())
    out_specs = (P(AXES), P(AXES))
    return jax.shard_map(
        functools.partial(body, row_bits, col_bits, owners, group_size),
        mesh=mesh,
        in_specs=in_specs,
        out_specs=out_specs,
        check_vma=False,
    )
```
